32 devices in a mesh: grp: 4 (over y, x), space: 8 (over z, core).
Axes of the slice: x: 2, y: 2, z: 4, core: 2. Of those that a mesh axis runs over, the one named last changes fastest.
Arguments:
- features: bfloat16 [4, 128, 128, 128], P('grp', 'space'), may hold values from -6 to 6
- weights: bfloat16 [27, 128, 128], replicated, may hold values from -0.109375 to 0.109375
- cotangent: bfloat16 [4, 128, 128, 128], P('grp', 'space'), may hold values from -6 to 6
- kernel_map: int32 [4, 128, 27], P('grp', 'space'), may hold values from -1 to 127, as said below
- counts: int32 [4, 8], P('grp', 'space'), may hold values from 4 to 16
Outputs:
- output: bfloat16 [4, 128, 128, 128], P('grp', 'space')
- input_grad: bfloat16 [4, 128, 128, 128], P('grp', 'space')
- weight_grad: float32 [3456, 128], P('space')
The draws below stay inside these ranges and needn't reach their ends.
Inputs may be any that keep to these rules, and one draw needn't show every extreme that they name: `kernel_map`: the centre offset k = 27 div 2 maps every block to itself. Otherwise an entry for an output block b on slab d = b div 16 is -1 or lies in [d * 16 - 4, (d + 1) * 16 + 4) within the sample. The live blocks of a device are its first counts slots.
All inputs are finite; a program needn't handle non-finite values.
Results may differ from the reference program's by a relative error of at most 0.005.
Values may be sent and summed in bfloat16 or wider, within the bound.
A program may use at most 64 MiB of HBM per device.

```python
import jax
import jax.numpy as jnp
from jax import lax

ROWS = 128
CIN = 128
COUT = 128
K = 27
H = 4
NB = 16
BLOCKS = 128
N_GRP = 4
N_SPACE = 8


def draw_kernel_map(key, part):
    block_ids = jnp.arange(BLOCKS, dtype=jnp.int32)
    slab = block_ids // NB
    lowest = jnp.maximum(slab * NB - H, 0)
    highest = jnp.minimum((slab + 1) * NB + H, BLOCKS)
    first_key, second_key = jax.random.split(jax.random.fold_in(key, 11))
    raw = jax.random.randint(first_key, (N_GRP, BLOCKS, K), 0, 1 << 20)
    source = lowest[None, :, None] + raw % (highest - lowest)[None, :, None]
    keep = jax.random.randint(second_key, (N_GRP, BLOCKS, K), 0, 10) < 7
    source = jnp.where(keep, source, -1)
    centre = jnp.arange(K, dtype=jnp.int32) == K // 2
    source = jnp.where(centre[None, None, :], block_ids[None, :, None], source)
    return source.astype(jnp.int32)


def plant(drawn, rng, low, high):
    longest = drawn.shape.index(max(drawn.shape))
    spots = []
    for shift in (0, 1):
        where = [jax.random.randint(jax.random.fold_in(rng, axis), (), 0, length) for axis, length in enumerate(drawn.shape)]
        where[longest] = (where[longest] + shift) % drawn.shape[longest]
        spots.append(tuple(where))
    return drawn.at[spots[0]].set(low).at[spots[1]].set(high)


def block_scale(key, shape, cuts, smallest, largest):
    def one(dim, parts):
        heights = jax.random.uniform(jax.random.fold_in(jax.random.fold_in(key, 6), dim), (parts,), jnp.float32, smallest / len(cuts), largest / len(cuts))
        return jnp.repeat(jnp.exp(heights), shape[dim] // parts).reshape((-1,) + (1,) * (len(shape) - dim - 1))

    level = one(*cuts[0])
    for cut in cuts[1:]:
        level = level * one(*cut)
    return level


def noise(rng, dims, width, limit, cuts=(), kind=jnp.bfloat16):
    result = width * jax.random.normal(rng, dims, jnp.float32)
    if cuts:
        result = result * block_scale(rng, dims, cuts, -0.22, 0.18)
    return jnp.clip(result, -limit, limit).astype(kind)


def setup_inputs(seed: int = 0) -> dict:
    splits = jax.random.split(jax.random.key(seed), 6)
    return {
        "features": noise(splits[0], (N_GRP, BLOCKS, ROWS, CIN), 1.0, 6.0, ((0, 4), (1, 8))),
        "weights": noise(splits[1], (K, CIN, COUT), (K * CIN) ** -0.5, 0.109375),
        "cotangent": noise(splits[2], (N_GRP, BLOCKS, ROWS, COUT), 1.0, 6.0, ((0, 4), (1, 8))),
        "kernel_map": draw_kernel_map(jax.random.fold_in(splits[5], 71), 0),
        "counts": plant(jax.random.randint(splits[4], (N_GRP, N_SPACE), NB // 4, NB + 1), jax.random.fold_in(splits[4], 1), NB // 4, NB).astype(jnp.int32),
    }


def reference(features, weights, cotangent, kernel_map, counts):
    block_ids = jnp.arange(BLOCKS, dtype=jnp.int32)
    outputs = []
    input_grads = []
    weight_grad = jnp.zeros((K, CIN, COUT), jnp.float32)
    for group in range(N_GRP):
        slab_counts = jnp.take(counts[group], block_ids // NB, axis=0)
        live_mask = ((block_ids % NB) < slab_counts).astype(jnp.bfloat16)[:, None, None]
        masked = features[group] * live_mask
        grad_out = cotangent[group] * live_mask
        block_map = kernel_map[group]
        present = (block_map >= 0).astype(jnp.bfloat16)
        source = jnp.maximum(block_map, 0).astype(jnp.int32)

        def step(offset, carry):
            total, grad_in, wgrad = carry
            column = lax.dynamic_index_in_dim(source, offset, 1, keepdims=False)
            present_k = lax.dynamic_index_in_dim(present, offset, 1, keepdims=False)[:, None, None]
            gathered = jnp.take(masked, column, axis=0) * present_k
            kernel = lax.dynamic_index_in_dim(weights, offset, 0, keepdims=False)
            total = total + jnp.einsum('brc,co->bro', gathered, kernel, preferred_element_type=jnp.float32)
            term = jnp.einsum('bro,co->brc', grad_out, kernel, preferred_element_type=jnp.float32)
            grad_in = grad_in.at[column].add(term * present_k.astype(jnp.float32))
            piece = jnp.einsum('brc,bro->co', gathered, grad_out, preferred_element_type=jnp.float32)
            wgrad = lax.dynamic_update_index_in_dim(wgrad, lax.dynamic_index_in_dim(wgrad, offset, 0, keepdims=False) + piece, offset, 0)
            return total, grad_in, wgrad

        start = (jnp.zeros((BLOCKS, ROWS, COUT), jnp.float32), jnp.zeros((BLOCKS, ROWS, CIN), jnp.float32), weight_grad)
        total, grad_in, weight_grad = lax.fori_loop(0, K, step, start)
        live_float = live_mask.astype(jnp.float32)
        outputs.append((total * live_float).astype(jnp.bfloat16))
        input_grads.append((grad_in * live_float).astype(jnp.bfloat16))
    return jnp.stack(outputs), jnp.stack(input_grads), weight_grad.reshape(K * CIN, COUT)
```

```python
import functools

import jax
import jax.numpy as jnp
from jax import lax
from jax.experimental import pallas as pl
from jax.experimental.pallas import tpu as pltpu
from jax.sharding import PartitionSpec as P

H = 4
BF16, F32 = jnp.bfloat16, jnp.float32
VMEM = pl.BlockSpec(memory_space=pltpu.VMEM)
SMEM = pl.BlockSpec(memory_space=pltpu.SMEM)


def fill_extended(ext, low, own, high, change=lambda x: x):
    slots = own.shape[0]
    for i in range(H):
        ext[i] = change(low[i])
        ext[H + slots + i] = change(high[i])
    for i in range(slots):
        ext[H + i] = change(own[i])
    ext[2 * H + slots] = jnp.zeros(ext.shape[1:], ext.dtype)


def input_grad_kernel(idx, cot, w, rims, own, acc):
    slots = cot.shape[0]
    offsets = idx.shape[1]
    cin = acc.shape[2]

    def clear(i, carry):
        acc[i] = jnp.zeros(acc.shape[1:], F32)
        return carry

    lax.fori_loop(0, acc.shape[0], clear, 0)

    def body(b, carry):
        g = cot[b]
        for k in range(0, offsets, 2):
            n = min(2, offsets - k)
            term = lax.dot_general(
                g, w[k * cin : (k + n) * cin], (((1,), (1,)), ((), ())), preferred_element_type=F32
            )
            for j in range(n):
                a = idx[b, k + j]
                acc[a] = acc[a] + term[:, j * cin : (j + 1) * cin]
        return carry

    lax.fori_loop(0, slots, body, 0)
    for i in range(H):
        rims[0, i] = acc[i].astype(BF16)
        rims[1, i] = acc[H + slots + i].astype(BF16)
    for i in range(slots):
        own[i] = acc[H + i]


def weight_grad_kernel(idx, low, feat, high, cot, part, ext):
    slots = feat.shape[0]
    offsets = idx.shape[1]
    cin = feat.shape[2]
    group = 3 if offsets % 3 == 0 else 1
    fill_extended(ext, low, feat, high, lambda x: x.T)
    def body(i, carry):
        rows = [
            jnp.concatenate([ext[idx[b, i * group + j]] for b in range(slots)], axis=1)
            for j in range(group)
        ]
        got = jnp.dot(jnp.concatenate(rows, axis=0), cot[...], preferred_element_type=F32)
        part[pl.ds(pl.multiple_of(i * group * cin, group * cin), group * cin), :] = got.astype(BF16)
        return carry

    lax.fori_loop(0, offsets // group, body, 0)


def window_start(g, groups, unit, rows):
    return pl.multiple_of(g * unit - (g // (groups - 1)) * (groups * unit - rows), 16)


def reduce_kernel(
    groups, space, unit,
    idx, live, low, feat, high, w, part, rims, own,
    out, ig, wg,
    ext, r0, p1, r1, p2, r2, r3, from_below, from_above,
    s0, q0, s1, q1, s2, q2, s3, q3, sr, qr,
):
    g = lax.axis_index("grp")
    s = lax.axis_index("space")
    half = space // 2
    z, c = s // 2, s % 2
    slots = feat.shape[0]
    offsets = idx.shape[1]
    rows = part.shape[2]
    partner = (g, z * 2 + (1 - c))
    grp_peers = [((g + d) % groups, s) for d in range(1, groups)]
    z_peers = [(g, ((z + d) % half) * 2 + c) for d in range(1, half)]

    barrier = pltpu.get_barrier_semaphore()
    fixed = [partner] + grp_peers + z_peers
    for peer in fixed:
        pl.semaphore_signal(barrier, inc=1, device_id=peer, device_id_type=pl.DeviceIdType.MESH)

    across = s - 1 + 2 * c
    has_across = jnp.logical_and(across >= 0, across < space)

    @pl.when(has_across)
    def _():
        pl.semaphore_signal(barrier, inc=1, device_id=(g, across), device_id_type=pl.DeviceIdType.MESH)

    fill_extended(ext, low, feat, high)
    pl.semaphore_wait(barrier, len(fixed) + has_across.astype(jnp.int32))

    def remote(src, dst, send, recv, peer):
        return pltpu.make_async_remote_copy(
            src_ref=src, dst_ref=dst, send_sem=send, recv_sem=recv,
            device_id=peer, device_id_type=pl.DeviceIdType.MESH,
        )

    copy0 = remote(part.at[:, 1 - c], r0, s0, q0, partner)
    copy0.start()
    down = remote(rims.at[0], from_above, sr.at[0], qr.at[0], (g, s - 1))
    up = remote(rims.at[1], from_below, sr.at[1], qr.at[1], (g, s + 1))

    @pl.when(s > 0)
    def _():
        down.start()

    @pl.when(s < space - 1)
    def _():
        up.start()

    pairs = slots // 2

    def forward(i, carry):
        rows_of = [
            jnp.concatenate([ext[idx[2 * i + j, k]] for k in range(offsets)], axis=1)
            for j in range(2)
        ]
        got = jnp.dot(jnp.concatenate(rows_of, axis=0), w[...], preferred_element_type=F32)
        n = feat.shape[1]
        for j in range(2):
            out[2 * i + j] = got[j * n : (j + 1) * n].astype(BF16)
        return carry

    def forward_part(q):
        lax.fori_loop(q * pairs // 4, (q + 1) * pairs // 4, forward, 0)

    forward_part(0)
    copy0.wait_recv()
    for i in range(half):
        p1[i] = (part[i, c].astype(F32) + r0[i].astype(F32)).astype(BF16)

    copies1 = []
    for d in range(1, groups):
        there = window_start((g + d) % groups, groups, unit, rows)
        copies1.append(
            remote(p1.at[:, pl.ds(there, unit)], r1.at[d - 1], s1.at[d - 1], q1.at[d - 1], grp_peers[d - 1])
        )
        copies1[-1].start()
    forward_part(1)
    for copy in copies1:
        copy.wait_recv()
    here = window_start(g, groups, unit, rows)
    for i in range(half):
        total = p1[i, pl.ds(here, unit), :].astype(F32)
        for d in range(1, groups):
            total = total + r1[d - 1, i].astype(F32)
        p2[i] = total.astype(BF16)

    copies2 = []
    for d in range(1, half):
        copies2.append(
            remote(p2.at[(z + d) % half], r2.at[d - 1], s2.at[d - 1], q2.at[d - 1], z_peers[d - 1])
        )
        copies2[-1].start()
    forward_part(2)
    for copy in copies2:
        copy.wait_recv()
    total = p2[z].astype(F32)
    for d in range(1, half):
        total = total + r2[d - 1].astype(F32)
    r3[0] = total

    copies3 = []
    for d in range(1, groups):
        copies3.append(remote(r3.at[0], r3.at[d], s3.at[d - 1], q3.at[d - 1], grp_peers[d - 1]))
        copies3[-1].start()
    forward_part(3)

    @pl.when(s < space - 1)
    def _():
        down.wait_recv()

    @pl.when(s > 0)
    def _():
        up.wait_recv()

    for i in range(slots):
        alive = jnp.where(i < live[0], 1.0, 0.0).astype(F32)
        value = own[i]
        if i < H:
            value = value + jnp.where(s > 0, from_below[i].astype(F32), 0.0)
        if i >= slots - H:
            value = value + jnp.where(s < space - 1, from_above[i - slots + H].astype(F32), 0.0)
        ig[i] = (value * alive).astype(BF16)

    for copy in copies3:
        copy.wait_recv()
    for j in range(groups):
        first = min(j * unit, rows - unit)
        wg[first : first + unit, :] = r3[(g - j + groups) % groups]
    copy0.wait_send()
    for copy in copies1 + copies2 + copies3:
        copy.wait_send()

    @pl.when(s > 0)
    def _():
        down.wait_send()

    @pl.when(s < space - 1)
    def _():
        up.wait_send()


def per_device(features, weights, cotangent, kernel_map, counts):
    voxels = features[0]
    slots, height, cin = voxels.shape
    offsets, _, cout = weights.shape
    space = lax.axis_size("space")
    groups = lax.axis_size("grp")
    device = lax.axis_index("space")
    live = counts[0]
    block_map = kernel_map[0]
    local = block_map - (device * slots - H)
    nowhere = slots + 2 * H
    slot_ids = jnp.arange(slots, dtype=jnp.int32)[:, None]
    usable = (block_map >= 0) & (slot_ids < live[0]) & ((local - H < live[0]) | (local >= slots + H))
    idx = jnp.where(usable, local, nowhere).astype(jnp.int32)
    high_ids = jnp.arange(slots - H, slots)
    top = voxels[slots - H :] * (high_ids < live[0]).astype(BF16)[:, None, None]
    up_route = [(i, i + 1) for i in range(space - 1)]
    low = lax.ppermute(top, "space", up_route)
    high = lax.ppermute(voxels[:H], "space", [(b, a) for a, b in up_route])
    flat_w = weights.reshape(offsets * cin, cout)

    rims, own = pl.pallas_call(
        input_grad_kernel,
        out_shape=(
            jax.ShapeDtypeStruct((2, H, height, cin), BF16),
            jax.ShapeDtypeStruct((slots, height, cin), F32),
        ),
        in_specs=[SMEM, VMEM, VMEM],
        out_specs=(VMEM, VMEM),
        scratch_shapes=[pltpu.VMEM((nowhere + 1, height, cin), F32)],
        cost_estimate=pl.CostEstimate(
            flops=2 * slots * height * cin * cout * offsets, bytes_accessed=4_000_000, transcendentals=0
        ),
        name="input_grad",
    )(idx, cotangent[0], flat_w)

    part = pl.pallas_call(
        weight_grad_kernel,
        out_shape=jax.ShapeDtypeStruct((offsets * cin, cout), BF16),
        in_specs=[SMEM] + [VMEM] * 4,
        out_specs=VMEM,
        scratch_shapes=[pltpu.VMEM((nowhere + 1, cin, height), BF16)],
        cost_estimate=pl.CostEstimate(
            flops=2 * slots * height * cin * cout * offsets, bytes_accessed=4_000_000, transcendentals=0
        ),
        name="weight_grad",
    )(idx, low, voxels, high, cotangent[0].reshape(slots * height, cout))

    half = space // 2
    rows = offsets * cin // space
    padded = -(-rows // 16) * 16
    part = part.reshape(space, rows, cout)
    if padded != rows:
        part = jnp.pad(part, ((0, 0), (0, padded - rows), (0, 0)))
    part = part.reshape(half, 2, padded, cout)
    unit = -(-padded // (16 * groups)) * 16
    dma = pltpu.SemaphoreType.DMA
    output, input_grad, wg = pl.pallas_call(
        functools.partial(reduce_kernel, groups, space, unit),
        out_shape=(
            jax.ShapeDtypeStruct((slots, height, cout), BF16),
            jax.ShapeDtypeStruct((slots, height, cin), BF16),
            jax.ShapeDtypeStruct((padded, cout), F32),
        ),
        in_specs=[SMEM, SMEM] + [VMEM] * 7,
        out_specs=(VMEM, VMEM, VMEM),
        scratch_shapes=[
            pltpu.VMEM((nowhere + 1, height, cin), BF16),
            pltpu.VMEM((half, padded, cout), BF16),
            pltpu.VMEM((half, padded, cout), BF16),
            pltpu.VMEM((groups - 1, half, unit, cout), BF16),
            pltpu.VMEM((half, unit, cout), BF16),
            pltpu.VMEM((half - 1, unit, cout), BF16),
            pltpu.VMEM((groups, unit, cout), F32),
            pltpu.VMEM((H, height, cin), BF16),
            pltpu.VMEM((H, height, cin), BF16),
            dma, dma,
            dma((groups - 1,)), dma((groups - 1,)),
            dma((half - 1,)), dma((half - 1,)),
            dma((groups - 1,)), dma((groups - 1,)),
            dma((2,)), dma((2,)),
        ],
        compiler_params=pltpu.CompilerParams(collective_id=0, has_side_effects=True),
        name="reduce_forward",
    )(idx, live, low, voxels, high, flat_w, part, rims, own)
    return output[None], input_grad[None], wg[:rows]


def solution(mesh):
    in_specs = (
        P("grp", "space", None, None),
        P(),
        P("grp", "space", None, None),
        P("grp", "space", None),
        P("grp", "space"),
    )
    out_specs = (P("grp", "space", None, None), P("grp", "space", None, None), P("space", None))
    return jax.shard_map(
        per_device, mesh=mesh, in_specs=in_specs, out_specs=out_specs, check_vma=False
    )
```

```python
import functools

import jax
import jax.numpy as jnp
from jax import lax
from jax.experimental import pallas as pl
from jax.experimental.pallas import tpu as pltpu
from jax.sharding import PartitionSpec as P

H = 4
BF16, F32 = jnp.bfloat16, jnp.float32
VMEM = pl.BlockSpec(memory_space=pltpu.VMEM)
SMEM = pl.BlockSpec(memory_space=pltpu.SMEM)


def input_grad_kernel(where, counts, block_map, cot, feat, w, idx, top, rims, own, acc):
    slots = cot.shape[0]
    offsets = block_map.shape[1]
    cin = acc.shape[2]
    live = counts[0, 0]
    first = where[0] * slots - H
    nowhere = slots + 2 * H

    def clear(i, carry):
        acc[i] = jnp.zeros(acc.shape[1:], F32)
        return carry

    lax.fori_loop(0, acc.shape[0], clear, 0)

    def body(b, carry):
        g = cot[b]
        for k in range(0, offsets, 2):
            n = min(2, offsets - k)
            term = lax.dot_general(
                g, w[k * cin : (k + n) * cin], (((1,), (1,)), ((), ())), preferred_element_type=F32
            )
            for j in range(n):
                source = block_map[b, k + j]
                local = source - first
                dead = jnp.logical_and(local - H >= live, local < slots + H)
                skip = jnp.logical_or(jnp.logical_or(source < 0, b >= live), dead)
                a = jnp.where(skip, nowhere, local)
                idx[b, k + j] = a
                acc[a] = acc[a] + term[:, j * cin : (j + 1) * cin]
        return carry

    lax.fori_loop(0, slots, body, 0)
    for i in range(H):
        alive = jnp.where(slots - H + i < live, 1.0, 0.0).astype(BF16)
        top[i] = feat[slots - H + i] * alive
        rims[0, i] = acc[i].astype(BF16)
        rims[1, i] = acc[H + slots + i].astype(BF16)
    for i in range(slots):
        own[i] = acc[H + i]


def window_start(g, groups, unit, rows):
    return pl.multiple_of(g * unit - (g // (groups - 1)) * (groups * unit - rows), 16)


def main_kernel(
    groups, space, unit, rows, padded,
    idx, top, feat, w, cot, rims,
    out, below, above, wg,
    low, high, ext, turned, flat, part, r0, p1, r1, p2, r2, r3,
    sh, qh, sr, qr, s0, q0, s1, q1, s2, q2, s3, q3,
):
    g = lax.axis_index("grp")
    s = lax.axis_index("space")
    half = space // 2
    z, c = s // 2, s % 2
    slots, height, cin = feat.shape
    offsets = idx.shape[1]
    partner = (g, z * 2 + (1 - c))
    grp_peers = [((g + d) % groups, s) for d in range(1, groups)]
    z_peers = [(g, ((z + d) % half) * 2 + c) for d in range(1, half)]

    barrier = pltpu.get_barrier_semaphore()
    fixed = [partner] + grp_peers + z_peers
    for peer in fixed:
        pl.semaphore_signal(barrier, inc=1, device_id=peer, device_id_type=pl.DeviceIdType.MESH)
    across = s - 1 + 2 * c
    has_across = jnp.logical_and(across >= 0, across < space)

    @pl.when(has_across)
    def _():
        pl.semaphore_signal(barrier, inc=1, device_id=(g, across), device_id_type=pl.DeviceIdType.MESH)

    def place(i, block):
        ext[i] = block
        turned[i] = block.T

    for i in range(slots):
        place(H + i, feat[i])
    zero = jnp.zeros((height, cin), BF16)
    for i in [2 * H + slots]:
        place(i, zero)
    pl.semaphore_wait(barrier, len(fixed) + has_across.astype(jnp.int32))

    def remote(src, dst, send, recv, peer):
        return pltpu.make_async_remote_copy(
            src_ref=src, dst_ref=dst, send_sem=send, recv_sem=recv,
            device_id=peer, device_id_type=pl.DeviceIdType.MESH,
        )

    halo_down = remote(feat.at[pl.ds(0, H)], high, sh.at[0], qh.at[0], (g, s - 1))
    halo_up = remote(top, low, sh.at[1], qh.at[1], (g, s + 1))
    down = remote(rims.at[0], above, sr.at[0], qr.at[0], (g, s - 1))
    up = remote(rims.at[1], below, sr.at[1], qr.at[1], (g, s + 1))
    has_down, has_up = s > 0, s < space - 1

    @pl.when(has_down)
    def _():
        halo_down.start()

    @pl.when(has_up)
    def _():
        halo_up.start()

    @pl.when(has_down)
    def _():
        down.start()

    @pl.when(has_up)
    def _():
        up.start()

    @pl.when(has_down)
    def _():
        halo_up.wait_recv()
        for i in range(H):
            place(i, low[i])

    @pl.when(jnp.logical_not(has_down))
    def _():
        for i in range(H):
            place(i, zero)

    @pl.when(has_up)
    def _():
        halo_down.wait_recv()
        for i in range(H):
            place(H + slots + i, high[i])

    @pl.when(jnp.logical_not(has_up))
    def _():
        for i in range(H):
            place(H + slots + i, zero)

    group = 3 if offsets % 3 == 0 else 1
    steps = offsets // group
    span = group * cin
    direct = rows == padded

    def weight_step(i, carry):
        lhs = [
            jnp.concatenate([turned[idx[b, i * group + j]] for b in range(slots)], axis=1)
            for j in range(group)
        ]
        got = jnp.dot(jnp.concatenate(lhs, axis=0), cot[...], preferred_element_type=F32)
        at = pl.ds(pl.multiple_of(i * span, span), span)
        if direct:
            part[at, :] = got.astype(BF16)
        else:
            flat[at, :] = got
        return carry

    pairs = slots // 2

    def forward(i, carry):
        lhs = [
            jnp.concatenate([ext[idx[2 * i + j, k]] for k in range(offsets)], axis=1)
            for j in range(2)
        ]
        got = jnp.dot(jnp.concatenate(lhs, axis=0), w[...], preferred_element_type=F32)
        for j in range(2):
            out[2 * i + j] = got[j * height : (j + 1) * height].astype(BF16)
        return carry

    def piece(p):
        return pl.ds(pl.multiple_of(p * padded, 16), padded)

    done = 0
    if not direct:
        lax.fori_loop(0, steps, weight_step, 0)
        done = steps
        for p in range(space):
            part[p * padded : p * padded + rows, :] = flat[p * rows : (p + 1) * rows, :].astype(BF16)
            part[p * padded + rows : (p + 1) * padded, :] = jnp.zeros((padded - rows, part.shape[1]), BF16)

    here = window_start(g, groups, unit, padded)
    copies0, copies1 = [], []
    copies2, copies3 = [], []
    for t in range(half + 4):
        if t < half:
            need = max(done, -(-(t + 1) * 2 * rows // span))
            if need > done:
                lax.fori_loop(done, need, weight_step, 0)
                done = need
            copies0.append(remote(part.at[piece(2 * t + 1 - c)], r0.at[t], s0.at[t], q0.at[t], partner))
            copies0[t].start()
        else:
            q = t - half
            lax.fori_loop(q * pairs // 4, (q + 1) * pairs // 4, forward, 0)
        i = t - 1
        if 0 <= i < half:
            copies0[i].wait_recv()
            p1[i] = (part[piece(2 * i + c), :].astype(F32) + r0[i].astype(F32)).astype(BF16)
            copies1.append([])
            for d in range(1, groups):
                there = window_start((g + d) % groups, groups, unit, padded)
                copies1[i].append(
                    remote(p1.at[i, pl.ds(there, unit)], r1.at[i, d - 1], s1.at[i, d - 1], q1.at[i, d - 1], grp_peers[d - 1])
                )
                copies1[i][-1].start()
        i = t - 2
        if 0 <= i < half:
            total = p1[i, pl.ds(here, unit), :].astype(F32)
            for d in range(1, groups):
                copies1[i][d - 1].wait_recv()
                total = total + r1[i, d - 1].astype(F32)
            p2[i] = total.astype(BF16)
            copies2.append(remote(p2.at[i], r2.at[z], s2.at[i], q2.at[z], (g, 2 * i + c)))

            @pl.when(z != i)
            def _(i=i):
                copies2[i].start()

        if t == half + 2:
            r2[z] = p2[z]
            total = jnp.zeros((unit, wg.shape[1]), F32)
            for i in range(half):

                @pl.when(z != i)
                def _(i=i):
                    remote(p2.at[i], r2.at[i], s2.at[i], q2.at[i], (g, 2 * i + c)).wait_recv()

            for i in range(half):
                total = total + r2[i].astype(F32)
            r3[0] = total
            for d in range(1, groups):
                copies3.append(remote(r3.at[0], r3.at[d], s3.at[d - 1], q3.at[d - 1], grp_peers[d - 1]))
                copies3[-1].start()

    for copy in copies3:
        copy.wait_recv()
    for j in range(groups):
        at = min(j * unit, padded - unit)
        wg[at : at + unit, :] = r3[(g - j + groups) % groups]

    @pl.when(has_down)
    def _():
        up.wait_recv()
        halo_down.wait_send()
        down.wait_send()

    @pl.when(has_up)
    def _():
        down.wait_recv()
        halo_up.wait_send()
        up.wait_send()

    for copy in copies0 + sum(copies1, []) + copies3:
        copy.wait_send()
    for i in range(half):

        @pl.when(z != i)
        def _(i=i):
            copies2[i].wait_send()


def per_device(features, weights, cotangent, kernel_map, counts):
    voxels = features[0]
    slots, height, cin = voxels.shape
    offsets, _, cout = weights.shape
    space = lax.axis_size("space")
    groups = lax.axis_size("grp")
    device = lax.axis_index("space")
    nowhere = slots + 2 * H
    flat_w = weights.reshape(offsets * cin, cout)

    idx, top, rims, own = pl.pallas_call(
        input_grad_kernel,
        out_shape=(
            jax.ShapeDtypeStruct((slots, offsets), jnp.int32),
            jax.ShapeDtypeStruct((H, height, cin), BF16),
            jax.ShapeDtypeStruct((2, H, height, cin), BF16),
            jax.ShapeDtypeStruct((slots, height, cin), F32),
        ),
        in_specs=[SMEM, SMEM, SMEM, VMEM, VMEM, VMEM],
        out_specs=(SMEM, VMEM, VMEM, VMEM),
        scratch_shapes=[pltpu.VMEM((nowhere + 1, height, cin), F32)],
        name="input_grad",
    )(device.astype(jnp.int32).reshape(1), counts, kernel_map[0], cotangent[0], voxels, flat_w)

    half = space // 2
    rows = offsets * cin // space
    padded = -(-rows // 16) * 16
    unit = -(-padded // (16 * groups)) * 16
    dma = pltpu.SemaphoreType.DMA
    rim = jax.ShapeDtypeStruct((H, height, cin), BF16)
    output, below, above, wg = pl.pallas_call(
        functools.partial(main_kernel, groups, space, unit, rows, padded),
        out_shape=(
            jax.ShapeDtypeStruct((slots, height, cout), BF16),
            rim,
            rim,
            jax.ShapeDtypeStruct((padded, cout), F32),
        ),
        in_specs=[SMEM] + [VMEM] * 5,
        out_specs=(VMEM,) * 4,
        scratch_shapes=[
            pltpu.VMEM((H, height, cin), BF16),
            pltpu.VMEM((H, height, cin), BF16),
            pltpu.VMEM((nowhere + 1, height, cin), BF16),
            pltpu.VMEM((nowhere + 1, cin, height), BF16),
            pltpu.VMEM((offsets * cin if rows != padded else 8, cout), F32),
            pltpu.VMEM((space * padded, cout), BF16),
            pltpu.VMEM((half, padded, cout), BF16),
            pltpu.VMEM((half, padded, cout), BF16),
            pltpu.VMEM((half, groups - 1, unit, cout), BF16),
            pltpu.VMEM((half, unit, cout), BF16),
            pltpu.VMEM((half, unit, cout), BF16),
            pltpu.VMEM((groups, unit, cout), F32),
            dma((2,)), dma((2,)),
            dma((2,)), dma((2,)),
            dma((half,)), dma((half,)),
            dma((half, groups - 1)), dma((half, groups - 1)),
            dma((half,)), dma((half,)),
            dma((groups - 1,)), dma((groups - 1,)),
        ],
        compiler_params=pltpu.CompilerParams(collective_id=0, has_side_effects=True),
        name="main",
    )(idx, top, voxels, flat_w, cotangent[0].reshape(slots * height, cout), rims)
    alive = (jnp.arange(slots) < counts[0, 0])[:, None, None]
    output = output * alive.astype(BF16)
    below = jnp.where(device > 0, below.astype(F32), 0.0)
    above = jnp.where(device < space - 1, above.astype(F32), 0.0)
    gap = jnp.zeros((slots - H, height, cin), F32)
    own = own + jnp.concatenate([below, gap], axis=0) + jnp.concatenate([gap, above], axis=0)
    input_grad = (own * alive.astype(F32)).astype(BF16)
    return output[None], input_grad[None], wg[:rows]


def solution(mesh):
    in_specs = (
        P("grp", "space", None, None),
        P(),
        P("grp", "space", None, None),
        P("grp", "space", None),
        P("grp", "space"),
    )
    out_specs = (P("grp", "space", None, None), P("grp", "space", None, None), P("space", None))
    return jax.shard_map(
        per_device, mesh=mesh, in_specs=in_specs, out_specs=out_specs, check_vma=False
    )
```

```python
import functools

import jax
import jax.numpy as jnp
from jax import lax
from jax.experimental import pallas as pl
from jax.experimental.pallas import tpu as pltpu
from jax.sharding import PartitionSpec as P

H = 4
BF16, F32 = jnp.bfloat16, jnp.float32
VMEM = pl.BlockSpec(memory_space=pltpu.VMEM)
SMEM = pl.BlockSpec(memory_space=pltpu.SMEM)


def input_grad_kernel(where, counts, block_map, cot, feat, w, idx, top, rims, own, acc):
    slots = cot.shape[0]
    offsets = block_map.shape[1]
    cin = acc.shape[2]
    live = counts[0, 0]
    first = where[0] * slots - H
    nowhere = slots + 2 * H

    def clear(i, carry):
        acc[i] = jnp.zeros(acc.shape[1:], F32)
        return carry

    lax.fori_loop(0, acc.shape[0], clear, 0)

    height = cot.shape[1]
    both = 2

    def body(i, carry):
        g = jnp.concatenate([cot[i * both + h] for h in range(both)], axis=0)
        for k in range(0, offsets, 2):
            n = min(2, offsets - k)
            term = lax.dot_general(
                g, w[k * cin : (k + n) * cin], (((1,), (1,)), ((), ())), preferred_element_type=F32
            )
            for h in range(both):
                b = i * both + h
                for j in range(n):
                    source = block_map[b, k + j]
                    local = source - first
                    dead = jnp.logical_and(local - H >= live, local < slots + H)
                    skip = jnp.logical_or(jnp.logical_or(source < 0, b >= live), dead)
                    a = jnp.where(skip, nowhere, local)
                    idx[b, k + j] = a
                    acc[a] = acc[a] + term[h * height : (h + 1) * height, j * cin : (j + 1) * cin]
        return carry

    lax.fori_loop(0, slots // both, body, 0)
    for i in range(H):
        alive = jnp.where(slots - H + i < live, 1.0, 0.0).astype(BF16)
        top[i] = feat[slots - H + i] * alive
        rims[0, i] = acc[i].astype(BF16)
        rims[1, i] = acc[H + slots + i].astype(BF16)
    for i in range(slots):
        own[i] = acc[H + i]


def window_start(g, groups, unit, rows):
    return pl.multiple_of(g * unit - (g // (groups - 1)) * (groups * unit - rows), 16)


def main_kernel(
    groups, space, unit, rows, padded,
    idx, top, feat, rims, w_far, cot_far,
    out, below, above, wg,
    w, cot, low, high, ext, turned, flat, part, r0, p1, r1, p2, r2, r3,
    sl, sh, qh, sr, qr, s0, q0, s1, q1, s2, q2, s3, q3,
):
    g = lax.axis_index("grp")
    s = lax.axis_index("space")
    half = space // 2
    z, c = s // 2, s % 2
    slots, height, cin = feat.shape
    offsets = idx.shape[1]
    partner = (g, z * 2 + (1 - c))
    grp_peers = [((g + d) % groups, s) for d in range(1, groups)]
    z_peers = [(g, ((z + d) % half) * 2 + c) for d in range(1, half)]

    barrier = pltpu.get_barrier_semaphore()
    fixed = [partner] + grp_peers + z_peers
    for peer in fixed:
        pl.semaphore_signal(barrier, inc=1, device_id=peer, device_id_type=pl.DeviceIdType.MESH)
    across = s - 1 + 2 * c
    has_across = jnp.logical_and(across >= 0, across < space)

    @pl.when(has_across)
    def _():
        pl.semaphore_signal(barrier, inc=1, device_id=(g, across), device_id_type=pl.DeviceIdType.MESH)

    def place(i, block):
        ext[i] = block
        turned[i] = block.T

    load_cot = pltpu.make_async_copy(cot_far, cot, sl.at[0])
    load_w = pltpu.make_async_copy(w_far, w, sl.at[1])
    load_cot.start()
    load_w.start()
    pl.semaphore_wait(barrier, len(fixed) + has_across.astype(jnp.int32))

    def remote(src, dst, send, recv, peer):
        return pltpu.make_async_remote_copy(
            src_ref=src, dst_ref=dst, send_sem=send, recv_sem=recv,
            device_id=peer, device_id_type=pl.DeviceIdType.MESH,
        )

    halo_down = remote(feat.at[pl.ds(0, H)], high, sh.at[0], qh.at[0], (g, s - 1))
    halo_up = remote(top, low, sh.at[1], qh.at[1], (g, s + 1))
    down = remote(rims.at[0], above, sr.at[0], qr.at[0], (g, s - 1))
    up = remote(rims.at[1], below, sr.at[1], qr.at[1], (g, s + 1))
    has_down, has_up = s > 0, s < space - 1

    @pl.when(has_down)
    def _():
        halo_down.start()

    @pl.when(has_up)
    def _():
        halo_up.start()

    for i in range(slots):
        place(H + i, feat[i])
    zero = jnp.zeros((height, cin), BF16)
    place(2 * H + slots, zero)

    @pl.when(has_down)
    def _():
        halo_up.wait_recv()
        for i in range(H):
            place(i, low[i])

    @pl.when(jnp.logical_not(has_down))
    def _():
        for i in range(H):
            place(i, zero)

    @pl.when(has_up)
    def _():
        halo_down.wait_recv()
        for i in range(H):
            place(H + slots + i, high[i])

    @pl.when(jnp.logical_not(has_up))
    def _():
        for i in range(H):
            place(H + slots + i, zero)

    @pl.when(has_down)
    def _():
        down.start()

    @pl.when(has_up)
    def _():
        up.start()

    load_cot.wait()
    group = 3 if offsets % 3 == 0 else 1
    steps = offsets // group
    span = group * cin
    direct = rows == padded

    def weight_step(i, carry):
        lhs = [
            jnp.concatenate([turned[idx[b, i * group + j]] for b in range(slots)], axis=1)
            for j in range(group)
        ]
        got = jnp.dot(jnp.concatenate(lhs, axis=0), cot[...], preferred_element_type=F32)
        at = pl.ds(pl.multiple_of(i * span, span), span)
        if direct:
            part[at, :] = got
        else:
            flat[at, :] = got
        return carry

    pairs = slots // 2

    def forward(i, carry):
        lhs = [
            jnp.concatenate([ext[idx[2 * i + j, k]] for k in range(offsets)], axis=1)
            for j in range(2)
        ]
        got = jnp.dot(jnp.concatenate(lhs, axis=0), w[...], preferred_element_type=F32)
        for j in range(2):
            out[2 * i + j] = got[j * height : (j + 1) * height].astype(BF16)
        return carry

    def piece(p):
        return pl.ds(pl.multiple_of(p * padded, 16), padded)

    done = 0
    if not direct:
        lax.fori_loop(0, steps, weight_step, 0)
        done = steps
        for p in range(space):
            part[p * padded : p * padded + rows, :] = flat[p * rows : (p + 1) * rows, :]
            part[p * padded + rows : (p + 1) * padded, :] = jnp.zeros((padded - rows, part.shape[1]), F32)

    here = window_start(g, groups, unit, padded)
    copies0, copies1 = [], []
    copies2, copies3 = [], []
    for t in range(half + 4):
        if t < half:
            need = max(done, -(-(t + 1) * 2 * rows // span))
            if need > done:
                lax.fori_loop(done, need, weight_step, 0)
                done = need
            copies0.append(remote(part.at[piece(2 * t + 1 - c)], r0.at[t], s0.at[t], q0.at[t], partner))
            copies0[t].start()
        else:
            q = t - half
            if q == 0:
                load_w.wait()
            lax.fori_loop(q * pairs // 4, (q + 1) * pairs // 4, forward, 0)
        i = t - 1
        if 0 <= i < half:
            copies0[i].wait_recv()
            p1[i] = (part[piece(2 * i + c), :] + r0[i]).astype(BF16)
            copies1.append([])
            for d in range(1, groups):
                there = window_start((g + d) % groups, groups, unit, padded)
                copies1[i].append(
                    remote(p1.at[i, pl.ds(there, unit)], r1.at[i, d - 1], s1.at[i, d - 1], q1.at[i, d - 1], grp_peers[d - 1])
                )
                copies1[i][-1].start()
        i = t - 2
        if 0 <= i < half:
            total = p1[i, pl.ds(here, unit), :].astype(F32)
            for d in range(1, groups):
                copies1[i][d - 1].wait_recv()
                total = total + r1[i, d - 1].astype(F32)
            p2[i] = total.astype(BF16)
            copies2.append(remote(p2.at[i], r2.at[z], s2.at[i], q2.at[z], (g, 2 * i + c)))

            @pl.when(z != i)
            def _(i=i):
                copies2[i].start()

        if t == half + 2:
            r2[z] = p2[z]
            total = jnp.zeros((unit, wg.shape[1]), F32)
            for i in range(half):

                @pl.when(z != i)
                def _(i=i):
                    remote(p2.at[i], r2.at[i], s2.at[i], q2.at[i], (g, 2 * i + c)).wait_recv()

            for i in range(half):
                total = total + r2[i].astype(F32)
            r3[0] = total.astype(BF16)
            for d in range(1, groups):
                copies3.append(remote(r3.at[0], r3.at[d], s3.at[d - 1], q3.at[d - 1], grp_peers[d - 1]))
                copies3[-1].start()

    for copy in copies3:
        copy.wait_recv()
    for j in range(groups):
        at = min(j * unit, padded - unit)
        wg[at : at + unit, :] = r3[(g - j + groups) % groups].astype(F32)

    @pl.when(has_down)
    def _():
        up.wait_recv()
        halo_down.wait_send()
        down.wait_send()

    @pl.when(has_up)
    def _():
        down.wait_recv()
        halo_up.wait_send()
        up.wait_send()

    for copy in copies0 + sum(copies1, []) + copies3:
        copy.wait_send()
    for i in range(half):

        @pl.when(z != i)
        def _(i=i):
            copies2[i].wait_send()


def finish_kernel(space, where, counts, raw, own, below, above, wg_in, out, ig, wg):
    slots = raw.shape[0]
    device = where[0]
    for i in range(slots):
        alive = jnp.where(i < counts[0, 0], 1.0, 0.0).astype(F32)
        value = own[i]
        if i < H:
            value = value + jnp.where(device > 0, below[i].astype(F32), 0.0)
        if i >= slots - H:
            value = value + jnp.where(device < space - 1, above[i - slots + H].astype(F32), 0.0)
        ig[i] = (value * alive).astype(BF16)
        out[i] = raw[i] * alive.astype(BF16)
    wg[...] = wg_in[: wg.shape[0], :]


def per_device(features, weights, cotangent, kernel_map, counts):
    voxels = features[0]
    slots, height, cin = voxels.shape
    offsets, _, cout = weights.shape
    space = lax.axis_size("space")
    groups = lax.axis_size("grp")
    device = lax.axis_index("space")
    position = device.astype(jnp.int32).reshape(1)
    nowhere = slots + 2 * H
    flat_w = weights.reshape(offsets * cin, cout)

    idx, top, rims, own = pl.pallas_call(
        input_grad_kernel,
        out_shape=(
            jax.ShapeDtypeStruct((slots, offsets), jnp.int32),
            jax.ShapeDtypeStruct((H, height, cin), BF16),
            jax.ShapeDtypeStruct((2, H, height, cin), BF16),
            jax.ShapeDtypeStruct((slots, height, cin), F32),
        ),
        in_specs=[SMEM, SMEM, SMEM, VMEM, VMEM, VMEM],
        out_specs=(SMEM, VMEM, VMEM, VMEM),
        scratch_shapes=[pltpu.VMEM((nowhere + 1, height, cin), F32)],
        name="input_grad",
    )(position, counts, kernel_map[0], cotangent[0], voxels, flat_w)

    half = space // 2
    rows = offsets * cin // space
    padded = -(-rows // 16) * 16
    unit = -(-padded // (16 * groups)) * 16
    dma = pltpu.SemaphoreType.DMA
    rim = jax.ShapeDtypeStruct((H, height, cin), BF16)
    output, below, above, wg = pl.pallas_call(
        functools.partial(main_kernel, groups, space, unit, rows, padded),
        out_shape=(
            jax.ShapeDtypeStruct((slots, height, cout), BF16),
            rim,
            rim,
            jax.ShapeDtypeStruct((padded, cout), F32),
        ),
        in_specs=[SMEM] + [VMEM] * 3 + [pl.BlockSpec(memory_space=pl.ANY)] * 2,
        out_specs=(VMEM,) * 4,
        scratch_shapes=[
            pltpu.VMEM((offsets * cin, cout), BF16),
            pltpu.VMEM((slots * height, cout), BF16),
            pltpu.VMEM((H, height, cin), BF16),
            pltpu.VMEM((H, height, cin), BF16),
            pltpu.VMEM((nowhere + 1, height, cin), BF16),
            pltpu.VMEM((nowhere + 1, cin, height), BF16),
            pltpu.VMEM((offsets * cin if rows != padded else 8, cout), F32),
            pltpu.VMEM((space * padded, cout), F32),
            pltpu.VMEM((half, padded, cout), F32),
            pltpu.VMEM((half, padded, cout), BF16),
            pltpu.VMEM((half, groups - 1, unit, cout), BF16),
            pltpu.VMEM((half, unit, cout), BF16),
            pltpu.VMEM((half, unit, cout), BF16),
            pltpu.VMEM((groups, unit, cout), BF16),
            dma((2,)),
            dma((2,)), dma((2,)),
            dma((2,)), dma((2,)),
            dma((half,)), dma((half,)),
            dma((half, groups - 1)), dma((half, groups - 1)),
            dma((half,)), dma((half,)),
            dma((groups - 1,)), dma((groups - 1,)),
        ],
        compiler_params=pltpu.CompilerParams(collective_id=0, has_side_effects=True),
        name="main",
    )(idx, top, voxels, rims, flat_w, cotangent[0].reshape(slots * height, cout))
    output, input_grad, wg = pl.pallas_call(
        functools.partial(finish_kernel, space),
        out_shape=(
            jax.ShapeDtypeStruct((slots, height, cout), BF16),
            jax.ShapeDtypeStruct((slots, height, cin), BF16),
            jax.ShapeDtypeStruct((rows, cout), F32),
        ),
        in_specs=[SMEM, SMEM] + [VMEM] * 5,
        out_specs=(VMEM,) * 3,
        name="finish",
    )(position, counts, output, own, below, above, wg)
    return output[None], input_grad[None], wg


def solution(mesh):
    in_specs = (
        P("grp", "space", None, None),
        P(),
        P("grp", "space", None, None),
        P("grp", "space", None),
        P("grp", "space"),
    )
    out_specs = (P("grp", "space", None, None), P("grp", "space", None, None), P("space", None))
    return jax.shard_map(
        per_device, mesh=mesh, in_specs=in_specs, out_specs=out_specs, check_vma=False
    )
```

```python
import functools

import jax
import jax.numpy as jnp
from jax import lax
from jax.experimental import pallas as pl
from jax.experimental.pallas import tpu as pltpu
from jax.sharding import PartitionSpec as P

H = 4
BF16, F32 = jnp.bfloat16, jnp.float32
VMEM = pl.BlockSpec(memory_space=pltpu.VMEM)
FAR = pl.BlockSpec(memory_space=pl.ANY)
SMEM = pl.BlockSpec(memory_space=pltpu.SMEM)


def input_grad_kernel(where, counts, block_map, cot, feat, w, idx, top, rims, own, acc):
    slots = cot.shape[0]
    offsets = block_map.shape[1]
    cin = acc.shape[2]
    live = counts[0, 0]
    first = where[0] * slots - H
    nowhere = slots + 2 * H

    def clear(i, carry):
        acc[i] = jnp.zeros(acc.shape[1:], F32)
        return carry

    lax.fori_loop(0, acc.shape[0], clear, 0)

    height = cot.shape[1]
    both = 4 if slots % 4 == 0 else 2

    def body(i, carry):
        g = jnp.concatenate([cot[i * both + h] for h in range(both)], axis=0)
        for k in range(0, offsets, 2):
            n = min(2, offsets - k)
            term = lax.dot_general(
                g, w[k * cin : (k + n) * cin], (((1,), (1,)), ((), ())), preferred_element_type=F32
            )
            for h in range(both):
                b = i * both + h
                for j in range(n):
                    source = block_map[b, k + j]
                    local = source - first
                    dead = jnp.logical_and(local - H >= live, local < slots + H)
                    skip = jnp.logical_or(jnp.logical_or(source < 0, b >= live), dead)
                    a = jnp.where(skip, nowhere, local)
                    idx[b, k + j] = a
                    acc[a] = acc[a] + term[h * height : (h + 1) * height, j * cin : (j + 1) * cin]
        return carry

    lax.fori_loop(0, slots // both, body, 0)
    for i in range(H):
        alive = jnp.where(slots - H + i < live, 1.0, 0.0).astype(BF16)
        top[i] = feat[slots - H + i] * alive
        rims[0, i] = acc[i].astype(BF16)
        rims[1, i] = acc[H + slots + i].astype(BF16)
    for i in range(slots):
        own[i] = acc[H + i]


def window_start(g, groups, unit, rows):
    return pl.multiple_of(g * unit - (g // (groups - 1)) * (groups * unit - rows), 16)


def main_kernel(
    groups, space, unit, rows, padded,
    idx, top, feat, rims, w_far, cot_far,
    out, below, above, wg,
    w, cot, ext, turned, flat, part, r0, p1, r1, p2, r2, r3,
    sl, sh, qh, sr, qr, s0, q0, s1, q1, s2, q2, s3, q3,
):
    g = lax.axis_index("grp")
    s = lax.axis_index("space")
    half = space // 2
    z, c = s // 2, s % 2
    slots, height, cin = feat.shape
    offsets = idx.shape[1]
    partner = (g, z * 2 + (1 - c))
    grp_peers = [((g + d) % groups, s) for d in range(1, groups)]
    z_peers = [(g, ((z + d) % half) * 2 + c) for d in range(1, half)]

    barrier = pltpu.get_barrier_semaphore()
    fixed = [partner] + grp_peers + z_peers
    for peer in fixed:
        pl.semaphore_signal(barrier, inc=1, device_id=peer, device_id_type=pl.DeviceIdType.MESH)
    across = s - 1 + 2 * c
    has_across = jnp.logical_and(across >= 0, across < space)

    @pl.when(has_across)
    def _():
        pl.semaphore_signal(barrier, inc=1, device_id=(g, across), device_id_type=pl.DeviceIdType.MESH)

    def turn(i):
        turned[i] = ext[i].T

    load_feat = pltpu.make_async_copy(feat, ext.at[pl.ds(H, slots)], sl.at[2])
    load_feat.start()
    load_cot = pltpu.make_async_copy(cot_far, cot, sl.at[0])
    load_w = pltpu.make_async_copy(w_far, w, sl.at[1])
    load_cot.start()
    load_w.start()
    pl.semaphore_wait(barrier, len(fixed) + has_across.astype(jnp.int32))

    def remote(src, dst, send, recv, peer):
        return pltpu.make_async_remote_copy(
            src_ref=src, dst_ref=dst, send_sem=send, recv_sem=recv,
            device_id=peer, device_id_type=pl.DeviceIdType.MESH,
        )

    halo_down = remote(feat.at[pl.ds(0, H)], ext.at[pl.ds(H + slots, H)], sh.at[0], qh.at[0], (g, s - 1))
    halo_up = remote(top, ext.at[pl.ds(0, H)], sh.at[1], qh.at[1], (g, s + 1))
    down = remote(rims.at[0], above, sr.at[0], qr.at[0], (g, s - 1))
    up = remote(rims.at[1], below, sr.at[1], qr.at[1], (g, s + 1))
    has_down, has_up = s > 0, s < space - 1

    @pl.when(has_down)
    def _():
        halo_down.start()

    @pl.when(has_up)
    def _():
        halo_up.start()

    zero = jnp.zeros((height, cin), BF16)
    ext[2 * H + slots] = zero
    turned[2 * H + slots] = zero
    load_feat.wait()
    for i in range(slots):
        turn(H + i)

    @pl.when(has_down)
    def _():
        halo_up.wait_recv()
        for i in range(H):
            turn(i)

    @pl.when(jnp.logical_not(has_down))
    def _():
        for i in range(H):
            ext[i] = zero
            turned[i] = zero

    @pl.when(has_up)
    def _():
        halo_down.wait_recv()
        for i in range(H):
            turn(H + slots + i)

    @pl.when(jnp.logical_not(has_up))
    def _():
        for i in range(H):
            ext[H + slots + i] = zero
            turned[H + slots + i] = zero

    @pl.when(has_down)
    def _():
        down.start()

    @pl.when(has_up)
    def _():
        up.start()

    load_cot.wait()
    group = 3 if offsets % 3 == 0 else 1
    steps = offsets // group
    span = group * cin
    direct = rows == padded

    def weight_step(i, carry):
        lhs = [
            jnp.concatenate([turned[idx[b, i * group + j]] for b in range(slots)], axis=1)
            for j in range(group)
        ]
        got = jnp.dot(jnp.concatenate(lhs, axis=0), cot[...], preferred_element_type=F32)
        at = pl.ds(pl.multiple_of(i * span, span), span)
        if direct:
            part[at, :] = got
        else:
            flat[at, :] = got
        return carry

    pairs = slots // 2

    def forward(i, carry):
        lhs = [
            jnp.concatenate([ext[idx[2 * i + j, k]] for k in range(offsets)], axis=1)
            for j in range(2)
        ]
        got = jnp.dot(jnp.concatenate(lhs, axis=0), w[...], preferred_element_type=F32)
        for j in range(2):
            out[2 * i + j] = got[j * height : (j + 1) * height].astype(BF16)
        return carry

    def piece(p):
        return pl.ds(pl.multiple_of(p * padded, 16), padded)

    done = 0
    if not direct:
        lax.fori_loop(0, steps, weight_step, 0)
        done = steps
        for p in range(space):
            part[p * padded : p * padded + rows, :] = flat[p * rows : (p + 1) * rows, :]
            part[p * padded + rows : (p + 1) * padded, :] = jnp.zeros((padded - rows, part.shape[1]), F32)

    here = window_start(g, groups, unit, padded)
    copies0, copies1 = [], []
    copies2, copies3 = [], []
    for t in range(half + 4):
        if t < half:
            need = max(done, -(-(t + 1) * 2 * rows // span))
            if need > done:
                lax.fori_loop(done, need, weight_step, 0)
                done = need
            copies0.append(remote(part.at[piece(2 * t + 1 - c)], r0.at[t], s0.at[t], q0.at[t], partner))
            copies0[t].start()
        else:
            q = t - half
            if q == 0:
                load_w.wait()
            lax.fori_loop(q * pairs // 4, (q + 1) * pairs // 4, forward, 0)
        i = t - 1
        if 0 <= i < half:
            copies0[i].wait_recv()
            p1[i] = (part[piece(2 * i + c), :] + r0[i]).astype(BF16)
            copies1.append([])
            for d in range(1, groups):
                there = window_start((g + d) % groups, groups, unit, padded)
                copies1[i].append(
                    remote(p1.at[i, pl.ds(there, unit)], r1.at[i, d - 1], s1.at[i, d - 1], q1.at[i, d - 1], grp_peers[d - 1])
                )
                copies1[i][-1].start()
        i = t - 2
        if 0 <= i < half:
            total = p1[i, pl.ds(here, unit), :].astype(F32)
            for d in range(1, groups):
                copies1[i][d - 1].wait_recv()
                total = total + r1[i, d - 1].astype(F32)
            p2[i] = total.astype(BF16)
            copies2.append(remote(p2.at[i], r2.at[z], s2.at[i], q2.at[z], (g, 2 * i + c)))

            @pl.when(z != i)
            def _(i=i):
                copies2[i].start()

        if t == half + 2:
            r2[z] = p2[z]
            total = jnp.zeros((unit, wg.shape[1]), F32)
            for i in range(half):

                @pl.when(z != i)
                def _(i=i):
                    remote(p2.at[i], r2.at[i], s2.at[i], q2.at[i], (g, 2 * i + c)).wait_recv()

            for i in range(half):
                total = total + r2[i].astype(F32)
            r3[0] = total.astype(BF16)
            for d in range(1, groups):
                copies3.append(remote(r3.at[0], r3.at[d], s3.at[d - 1], q3.at[d - 1], grp_peers[d - 1]))
                copies3[-1].start()

    for copy in copies3:
        copy.wait_recv()
    for j in range(groups):
        at = min(j * unit, padded - unit)
        wg[at : at + unit, :] = r3[(g - j + groups) % groups].astype(F32)

    @pl.when(has_down)
    def _():
        up.wait_recv()
        halo_down.wait_send()
        down.wait_send()

    @pl.when(has_up)
    def _():
        down.wait_recv()
        halo_up.wait_send()
        up.wait_send()

    for copy in copies0 + sum(copies1, []) + copies3:
        copy.wait_send()
    for i in range(half):

        @pl.when(z != i)
        def _(i=i):
            copies2[i].wait_send()


def finish_kernel(
    space, where, counts, raw_far, own_far, below_far, above_far, wg_far, out_far, ig_far, wg_out,
    raw, own, below, above, wg_in, out, ig, wg, load, store,
):
    slots = raw.shape[0]
    device = where[0]
    parts = slots // H
    chunk = [pl.ds(q * H, H) for q in range(parts)]
    copy = pltpu.make_async_copy
    edges = [copy(below_far, below, load.at[2 * parts]), copy(above_far, above, load.at[2 * parts + 1])]
    sums = copy(wg_far, wg_in, load.at[2 * parts + 2])
    owns = [copy(own_far.at[chunk[q]], own.at[chunk[q]], load.at[q]) for q in range(parts)]
    raws = [copy(raw_far.at[chunk[q]], raw.at[chunk[q]], load.at[parts + q]) for q in range(parts)]
    for q in range(parts):
        owns[q].start()
        raws[q].start()
        if q == 0:
            for edge in edges:
                edge.start()
    sums.start()
    stores = []
    for q in range(parts):
        owns[q].wait()
        raws[q].wait()
        if q == 0:
            for edge in edges:
                edge.wait()
        for i in range(q * H, (q + 1) * H):
            alive = jnp.where(i < counts[0, 0], 1.0, 0.0).astype(F32)
            value = own[i]
            if i < H:
                value = value + jnp.where(device > 0, below[i].astype(F32), 0.0)
            if i >= slots - H:
                value = value + jnp.where(device < space - 1, above[i - slots + H].astype(F32), 0.0)
            ig[i] = (value * alive).astype(BF16)
            out[i] = raw[i] * alive.astype(BF16)
        stores.append(copy(ig.at[chunk[q]], ig_far.at[chunk[q]], store.at[q]))
        stores.append(copy(out.at[chunk[q]], out_far.at[chunk[q]], store.at[parts + q]))
        stores[-2].start()
        stores[-1].start()
    sums.wait()
    wg[...] = wg_in[: wg.shape[0], :]
    stores.append(copy(wg, wg_out, store.at[2 * parts]))
    stores[-1].start()
    for item in stores:
        item.wait()


def per_device(features, weights, cotangent, kernel_map, counts):
    voxels = features[0]
    slots, height, cin = voxels.shape
    offsets, _, cout = weights.shape
    space = lax.axis_size("space")
    groups = lax.axis_size("grp")
    device = lax.axis_index("space")
    position = device.astype(jnp.int32).reshape(1)
    nowhere = slots + 2 * H
    flat_w = weights.reshape(offsets * cin, cout)

    idx, top, rims, own = pl.pallas_call(
        input_grad_kernel,
        out_shape=(
            jax.ShapeDtypeStruct((slots, offsets), jnp.int32),
            jax.ShapeDtypeStruct((H, height, cin), BF16),
            jax.ShapeDtypeStruct((2, H, height, cin), BF16),
            jax.ShapeDtypeStruct((slots, height, cin), F32),
        ),
        in_specs=[SMEM, SMEM, SMEM, VMEM, VMEM, VMEM],
        out_specs=(SMEM, VMEM, VMEM, VMEM),
        scratch_shapes=[pltpu.VMEM((nowhere + 1, height, cin), F32)],
        name="input_grad",
    )(position, counts, kernel_map[0], cotangent[0], voxels, flat_w)

    half = space // 2
    rows = offsets * cin // space
    padded = -(-rows // 16) * 16
    unit = -(-padded // (16 * groups)) * 16
    dma = pltpu.SemaphoreType.DMA
    rim = jax.ShapeDtypeStruct((H, height, cin), BF16)
    output, below, above, wg = pl.pallas_call(
        functools.partial(main_kernel, groups, space, unit, rows, padded),
        out_shape=(
            jax.ShapeDtypeStruct((slots, height, cout), BF16),
            rim,
            rim,
            jax.ShapeDtypeStruct((padded, cout), F32),
        ),
        in_specs=[SMEM] + [FAR] * 5,
        out_specs=(VMEM,) * 4,
        scratch_shapes=[
            pltpu.VMEM((offsets * cin, cout), BF16),
            pltpu.VMEM((slots * height, cout), BF16),
            pltpu.VMEM((nowhere + 1, height, cin), BF16),
            pltpu.VMEM((nowhere + 1, cin, height), BF16),
            pltpu.VMEM((offsets * cin if rows != padded else 8, cout), F32),
            pltpu.VMEM((space * padded, cout), F32),
            pltpu.VMEM((half, padded, cout), F32),
            pltpu.VMEM((half, padded, cout), BF16),
            pltpu.VMEM((half, groups - 1, unit, cout), BF16),
            pltpu.VMEM((half, unit, cout), BF16),
            pltpu.VMEM((half, unit, cout), BF16),
            pltpu.VMEM((groups, unit, cout), BF16),
            dma((3,)),
            dma((2,)), dma((2,)),
            dma((2,)), dma((2,)),
            dma((half,)), dma((half,)),
            dma((half, groups - 1)), dma((half, groups - 1)),
            dma((half,)), dma((half,)),
            dma((groups - 1,)), dma((groups - 1,)),
        ],
        compiler_params=pltpu.CompilerParams(collective_id=0, has_side_effects=True),
        name="main",
    )(idx, top, voxels, rims, flat_w, cotangent[0].reshape(slots * height, cout))
    output, input_grad, wg = pl.pallas_call(
        functools.partial(finish_kernel, space),
        out_shape=(
            jax.ShapeDtypeStruct((slots, height, cout), BF16),
            jax.ShapeDtypeStruct((slots, height, cin), BF16),
            jax.ShapeDtypeStruct((rows, cout), F32),
        ),
        in_specs=[SMEM, SMEM] + [FAR] * 5,
        out_specs=(FAR,) * 3,
        scratch_shapes=[
            pltpu.VMEM((slots, height, cout), BF16),
            pltpu.VMEM((slots, height, cin), F32),
            pltpu.VMEM((H, height, cin), BF16),
            pltpu.VMEM((H, height, cin), BF16),
            pltpu.VMEM((padded, cout), F32),
            pltpu.VMEM((slots, height, cout), BF16),
            pltpu.VMEM((slots, height, cin), BF16),
            pltpu.VMEM((rows, cout), F32),
            dma((2 * (slots // H) + 3,)),
            dma((2 * (slots // H) + 1,)),
        ],
        name="finish",
    )(position, counts, output, own, below, above, wg)
    return output[None], input_grad[None], wg


def solution(mesh):
    in_specs = (
        P("grp", "space", None, None),
        P(),
        P("grp", "space", None, None),
        P("grp", "space", None),
        P("grp", "space"),
    )
    out_specs = (P("grp", "space", None, None), P("grp", "space", None, None), P("space", None))
    return jax.shard_map(
        per_device, mesh=mesh, in_specs=in_specs, out_specs=out_specs, check_vma=False
    )
```
